128 devices in a mesh: dp: 16 (over x_lo, z, core), space: 8 (over x_hi, y).
Axes of the slice: x: 4 (x_hi: 2, x_lo: 2; x = x_hi * 2 + x_lo), y: 4, z: 4, core: 2. Of those that a mesh axis runs over, the one named last changes fastest.
Arguments:
- volume: bfloat16 [16, 4, 32, 32, 128], P('dp', None, 'space'), may hold values from -6 to 6
- w_first: bfloat16 [27, 32, 4], replicated, may hold values from -0.625 to 0.625
- b_first: float32 [32], replicated, may hold values from -3 to 3
- w_second: bfloat16 [27, 64, 32], replicated, may hold values from -0.21875 to 0.21875
- b_second: float32 [64], replicated, may hold values from -3 to 3
- cotangent: bfloat16 [16, 64, 8, 256], P('dp', None, 'space'), may hold values from -0.119628906 to 0.119628906
Outputs:
- pooled_out: bfloat16 [16, 64, 8, 256], P('dp', None, 'space')
- grad_w_first: float32 [27, 32, 4], replicated
- grad_b_first: float32 [32], replicated
- grad_w_second: float32 [27, 64, 32], replicated
- grad_b_second: float32 [64], replicated
The draws below stay inside these ranges and needn't reach their ends.
All inputs are finite; a program needn't handle non-finite values.
Results may differ from the reference program's by a relative error of at most 0.0049.
The reference program's roundings to bfloat16 on the way (of `pooled_one`, `delta_two` and `delta_one`) count: a program that leaves them out, or rounds other values in their place, can miss the bound.
Values may be sent and summed in bfloat16 or wider, within the bound.
A program may use at most 64 MiB of HBM per device.

```python
import jax
import jax.numpy as jnp
from jax import lax

C0 = 4
C1 = 32
C2 = 64
Y = 32
X = 128
B = 16
Z = 32


def level_of(rng, shape, cuts, smallest, largest):
    gain, own = 1.0, jax.random.fold_in(rng, 6)
    for dim, blocks in cuts:
        heights = jnp.exp(jax.random.uniform(jax.random.fold_in(own, dim), (blocks,), jnp.float32, smallest / len(cuts), largest / len(cuts)))
        gain = gain * jnp.repeat(heights, shape[dim] // blocks).reshape([-1 if axis == dim else 1 for axis in range(len(shape))])
    return gain


def gaussian(rng, shape, scale, limit, shards=(), kind=jnp.bfloat16):
    array = scale * jax.random.normal(rng, shape, jnp.float32)
    if shards:
        array = array * level_of(rng, shape, shards, -0.22, 0.18)
    return jnp.clip(array, -limit, limit).astype(kind)


def setup_inputs(seed: int = 0) -> dict:
    seeds = jax.random.split(jax.random.key(seed), 7)
    return {
        "volume": gaussian(seeds[0], (B, C0, Z, Y, X), 1.0, 6.0, ((0, 16), (2, 8))),
        "w_first": gaussian(seeds[1], (27, C1, C0), (27 * C0) ** -0.5, 0.625),
        "b_first": gaussian(seeds[2], (C1,), 0.5, 3.0, (), jnp.float32),
        "w_second": gaussian(seeds[3], (27, C2, C1), (27 * C1) ** -0.5, 0.21875),
        "b_second": gaussian(seeds[4], (C2,), 0.5, 3.0, (), jnp.float32),
        "cotangent": gaussian(seeds[5], (B, C2, Z // 4, (Y // 4) * (X // 4)), 0.02, 0.119628906, ((0, 16), (2, 8))),
    }


numbers = ('NCDHW', 'OIDHW', 'NCDHW')

def to_kernel(weight):
    outs_count = weight.shape[1]
    ins_count = weight.shape[2]
    return weight.astype(jnp.float32).reshape(3, 3, 3, outs_count, ins_count).transpose(3, 4, 0, 1, 2)

def convolve(field, kernel):
    return lax.conv_general_dilated(field[None], kernel, (1, 1, 1), ((1, 1), (1, 1), (1, 1)), dimension_numbers=numbers, precision=lax.Precision.HIGHEST)[0]

def from_kernel(kernel):
    return kernel.transpose(2, 3, 4, 0, 1).reshape(27, kernel.shape[0], kernel.shape[1])

def leaky_relu(field):
    return jnp.where(field > 0, field, 0.3 * field)

def slopes(field):
    return jnp.where(field > 0, 1.0, 0.3)

def pooling(field):
    lead = field.shape[:-3]
    depth_n, rows_n, cols_n = field.shape[-3:]
    return field.reshape(lead + (depth_n // 2, 2, rows_n // 2, 2, cols_n // 2, 2)).mean(axis=(-5, -3, -1))

def upsample(field):
    lead = field.shape[:-3]
    depth_n, rows_n, cols_n = field.shape[-3:]
    wide_field = jnp.broadcast_to(field[..., :, None, :, None, :, None], lead + (depth_n, 2, rows_n, 2, cols_n, 2))
    return wide_field.reshape(lead + (2 * depth_n, 2 * rows_n, 2 * cols_n))

def rounded(field):
    return lax.optimization_barrier(field.astype(jnp.bfloat16)).astype(jnp.float32)

def reference(volume, w_first, b_first, w_second, b_second, cotangent):
    kernel_one = to_kernel(w_first)
    kernel_two = to_kernel(w_second)

    def one_sample(carry, items):
        sample, grad_in = items
        source = sample.astype(jnp.float32)
        act_one = convolve(source, kernel_one) + b_first[:, None, None, None]
        pooled_one = rounded(pooling(leaky_relu(act_one)))
        act_two = convolve(pooled_one, kernel_two) + b_second[:, None, None, None]
        result = pooling(leaky_relu(act_two)).astype(jnp.bfloat16)
        shape_top = result.shape
        result = result.reshape(shape_top[0], shape_top[1], shape_top[2] * shape_top[3])
        grad_top = grad_in.astype(jnp.float32).reshape(shape_top)
        delta_two = rounded(upsample(grad_top) * 0.125 * slopes(act_two))
        unused, back_two = jax.vjp(convolve, pooled_one, kernel_two)
        back_one, kgrad_two = back_two(delta_two)
        delta_one = rounded(upsample(back_one) * 0.125 * slopes(act_one))
        unused_one, back_first = jax.vjp(lambda kernel: convolve(source, kernel), kernel_one)
        kgrad_one = back_first(delta_one)[0]
        new_carry = (carry[0] + from_kernel(kgrad_one), carry[1] + lax.optimization_barrier(jnp.sum(delta_one, axis=(1, 2, 3))), carry[2] + from_kernel(kgrad_two), carry[3] + lax.optimization_barrier(jnp.sum(delta_two, axis=(1, 2, 3))))
        return (new_carry, result)
    start = (jnp.zeros(w_first.shape, jnp.float32), jnp.zeros(b_first.shape, jnp.float32), jnp.zeros(w_second.shape, jnp.float32), jnp.zeros(b_second.shape, jnp.float32))
    sums, results = lax.scan(one_sample, start, (volume, cotangent))
    return (results, sums[0], sums[1], sums[2], sums[3])
```

```python
import functools

import jax
import jax.numpy as jnp
from jax import lax
from jax.experimental import pallas as pl
from jax.experimental.pallas import tpu as pltpu
from jax.sharding import PartitionSpec as P

MESH = pl.DeviceIdType.MESH
BF = jnp.bfloat16
F32 = jnp.float32

LANES = 256
COLS = 32
SLOTS = 28
TILES = 9


def dot(a, b):
    return jnp.dot(a, b, preferred_element_type=F32)


def dot_nt(a, b):
    return lax.dot_general(a, b, (((1,), (1,)), ((), ())), preferred_element_type=F32)


def lane_of(shape):
    return lax.broadcasted_iota(jnp.int32, shape, len(shape) - 1)


def shift_x(v, step):
    lane = lane_of(v.shape)
    moved = pltpu.roll(v, step % LANES, 1)
    edge = 0 if step == 1 else COLS - 1
    return jnp.where(lane % COLS == edge, 0.0, moved)


def shift_y(v, step):
    lane = lane_of(v.shape)
    moved = pltpu.roll(v, (step * COLS) % LANES, 1)
    gone = lane < COLS if step == 1 else lane >= LANES - COLS
    return jnp.where(gone, 0.0, moved)


def leaky(v):
    return jnp.where(v > 0, v, 0.3 * v)


def slope(v):
    return jnp.where(v > 0, 1.0, 0.3)


def column(row):
    n = row.shape[1]
    r = lax.broadcasted_iota(jnp.int32, (n, n), 0)
    c = lax.broadcasted_iota(jnp.int32, (n, n), 1)
    return jnp.sum(jnp.where(r == c, jnp.broadcast_to(row, (n, n)), 0.0), axis=1, keepdims=True)


def window_layer(out, layer, raw, chans, keep):
    wide = []
    for qy in range(2):
        even = raw(2 * qy).astype(F32)
        odd = raw(2 * qy + 1).astype(F32)
        if keep is not None:
            even = jnp.where(keep, even, 0.0)
            odd = jnp.where(keep, odd, 0.0)
        wide.append(jnp.concatenate([shift_x(odd, 1), even, odd, shift_x(even, -1)], axis=0))
    out[layer, 0] = shift_y(wide[1], 1).astype(BF)
    out[layer, 1] = wide[0].astype(BF)
    out[layer, 2] = wide[1].astype(BF)
    out[layer, 3] = shift_y(wide[0], -1).astype(BF)


def kernel(
    n_dp,
    n_sp,
    vol,
    w1t,
    b1,
    w2t,
    b2,
    cot,
    top_out,
    gw1_out,
    gb1_out,
    gw2_out,
    gb2_out,
    pick,
    halo_v,
    ext,
    base_w,
    w1p,
    w2p,
    w2f,
    act1,
    pooled,
    halo_p,
    win2,
    delta2,
    halo_d,
    win3,
    acc,
    g2,
    r2,
    s2,
    f2,
    g1,
    r1,
    s1,
    f1,
    halo_send,
    halo_recv,
    send_a2,
    recv_a2,
    send_b2,
    recv_b2,
    send_c2,
    recv_c2,
    send_a1,
    recv_a1,
    send_b1,
    recv_b1,
    send_c1,
    recv_c1,
):
    d = lax.axis_index("dp")
    s = lax.axis_index("space")
    left = lax.rem(s + n_sp - 1, n_sp)
    right = lax.rem(s + 1, n_sp)
    has_left = s > 0
    has_right = s < n_sp - 1

    barrier = pltpu.get_barrier_semaphore()
    for r in range(1, n_sp):
        pl.semaphore_signal(
            barrier, inc=1, device_id={"space": lax.rem(s + r, n_sp)}, device_id_type=MESH
        )
    for r in range(1, n_dp):
        pl.semaphore_signal(
            barrier, inc=1, device_id={"dp": lax.rem(d + r, n_dp)}, device_id_type=MESH
        )

    for f in range(6):
        r = lax.broadcasted_iota(jnp.int32, (128, LANES), 0)
        c = lane_of((128, LANES)) % COLS
        pick[:, f * LANES : (f + 1) * LANES] = jnp.where(r == 4 * c + f - 1, 1.0, 0.0).astype(BF)
    row = lax.broadcasted_iota(jnp.int32, (64, 512), 0)
    col = lax.broadcasted_iota(jnp.int32, (64, 512), 1)
    gather = jnp.where(
        (row // 16 == col % 4) & ((row % 16) // 4 == col // 128) & (row % 4 == (col % 128) // 32),
        1.0,
        0.0,
    ).astype(BF)
    own_y = (lax.broadcasted_iota(jnp.int32, (128, LANES), 0) % 32) // 4 == lane_of(
        (128, LANES)
    ) // COLS

    def volume_layer(layer, plane):
        parts = []
        for f in range(6):
            spread = dot(plane, pick[:, f * LANES : (f + 1) * LANES])
            parts.append(jnp.where(own_y, spread, 0.0).astype(BF))
        for qx in range(2):
            cells = dot(gather, jnp.concatenate(parts[2 * qx : 2 * qx + 4], axis=0))
            ext[qx, layer, 0] = shift_y(cells[48:64], 1).astype(BF)
            for fy in range(4):
                ext[qx, layer, fy + 1] = cells[16 * fy : 16 * fy + 16].astype(BF)
            ext[qx, layer, 5] = shift_y(cells[0:16], -1).astype(BF)

    def halo_copy(src, dst, sem, to):
        return pltpu.make_async_remote_copy(
            src_ref=src,
            dst_ref=dst,
            send_sem=halo_send.at[sem],
            recv_sem=halo_recv.at[sem],
            device_id={"space": to},
            device_id_type=MESH,
        )

    pl.semaphore_wait(barrier, n_sp - 1 + n_dp - 1)
    v_left = halo_copy(vol.at[:, 0], halo_v.at[1], 0, left)
    v_right = halo_copy(vol.at[:, 3], halo_v.at[0], 1, right)
    v_left.start()
    v_right.start()

    for z in range(4):
        volume_layer(z + 1, vol[:, z].reshape(128, 128))

    base_w[...] = jnp.zeros_like(base_w)
    for k in range(27):
        at = 4 * (16 * (k // 9) + 4 * ((k // 3) % 3) + k % 3)
        base_w[at : at + 4, 0:32] = w1t[k].astype(F32)
    base = base_w[...].T[0:32]
    for p in range(8):
        by = 4 * (16 * (p // 4) + 4 * ((p // 2) % 2) + p % 2)
        w1p[32 * p : 32 * p + 32] = (pltpu.roll(base, by, 1) if by else base).astype(BF)
    none = jnp.zeros((32, 64), F32)
    for ac in range(9):
        taps = [w2t[3 * ac + e].astype(F32) for e in range(3)]
        blocks = [
            jnp.concatenate([taps[w] if w < 3 else none, taps[w - 1] if w > 0 else none], axis=1)
            for w in range(4)
        ]
        w2p[:, 128 * ac : 128 * ac + 128] = jnp.concatenate(blocks, axis=0).T.astype(BF)
        at = 256 * (8 - ac)
        w2f[0:32, at : at + 256] = jnp.concatenate([taps[2], taps[1], taps[0], none], axis=1).astype(BF)
        w2f[32:64, at : at + 256] = jnp.concatenate([none, taps[2], taps[1], taps[0]], axis=1).astype(BF)
    b1c = column(b1[...])
    b2c = column(b2[...])

    v_left.wait()
    v_right.wait()
    for side, keep in ((0, has_left), (1, has_right)):
        plane = halo_v[side].reshape(128, 128).astype(F32)
        volume_layer(5 * side, jnp.where(keep, plane, 0.0).astype(BF))

    def first_window(q):
        qz, qy, qx = q // 4, (q // 2) % 2, q % 2
        return ext[qx, 2 * qz : 2 * qz + 4, 2 * qy : 2 * qy + 4].reshape(256, LANES)

    p_copies = []
    for qz in range(2):
        for qq in range(4):
            q = 4 * qz + qq
            act = dot(w1p[...], first_window(q)).reshape(8, 32, LANES) + b1c[None]
            act1[q] = act
            pooled[qz, qq] = (jnp.sum(leaky(act), axis=0) * 0.125).astype(BF)
        copy = halo_copy(pooled.at[qz], halo_p.at[1 - qz], 2 + qz, right if qz else left)
        copy.start()
        p_copies.append(copy)

    for qz in range(2):
        window_layer(win2, 1 + qz, lambda j, qz=qz: pooled[qz, j], 32, None)

    def second_window(pz, py, a0, a1):
        return win2[pz + a0 : pz + a1, py : py + 3].reshape((a1 - a0) * 384, LANES)

    for pz in range(2):
        for py in range(2):
            own = second_window(pz, py, 1 - pz, 3 - pz)
            acc[2 * pz + py] = dot(w2p[:, 384 * (1 - pz) : 384 * (3 - pz)], own)
    for copy in p_copies:
        copy.wait()
    grad_top = cot[...].astype(F32) * 0.125
    top = jnp.zeros((64, LANES), F32)
    d_copies = []
    for pz in range(2):
        keep = has_right if pz else has_left
        window_layer(win2, 3 * pz, lambda j, pz=pz: halo_p[pz, j], 32, keep)
        for py in range(2):
            at = 2 * pz
            act = acc[2 * pz + py] + dot(
                w2p[:, 384 * at : 384 * at + 384], second_window(pz, py, at, at + 1)
            )
            for px in range(2):
                one = act[64 * px : 64 * px + 64] + b2c
                top = top + leaky(one)
                delta2[pz, 2 * py + px] = (grad_top * slope(one)).astype(BF)
        copy = halo_copy(delta2.at[pz], halo_d.at[1 - pz], 4 + pz, right if pz else left)
        copy.start()
        d_copies.append(copy)
    top_out[...] = (top * 0.125).astype(BF)

    ones = jnp.ones((16, LANES), BF)
    grad = None
    sums = None
    for pz in range(2):
        for py in range(2):
            there = delta2[pz, 2 * py : 2 * py + 2].reshape(128, LANES)
            term = dot_nt(second_window(pz, py, 0, 3), there)
            part = dot_nt(ones, there)
            grad = term if grad is None else grad + term
            sums = part if sums is None else sums + part
    low = lane_of((16, 128)) < 64
    per2 = -(-SLOTS // n_dp)
    for k in range(27):
        at = 128 * (k // 3) + 32 * (k % 3)
        here, after = grad[at : at + 32], grad[at + 32 : at + 64]
        first = here[0:16] + pltpu.roll(after[0:16], 64, 1)
        second = pltpu.roll(here[16:32], 64, 1) + after[16:32]
        g2[k // per2, k % per2] = jnp.where(low, first, second)
    g2[27 // per2, 27 % per2] = sums + pltpu.roll(sums, 64, 1)
    for extra in range(SLOTS, per2 * (-(-SLOTS // per2))):
        g2[extra // per2, extra % per2] = jnp.zeros((16, 128), F32)

    def phase_a(src, land, send, recv, owners, start):
        for r in range(1, n_dp):
            to = lax.rem(d + r, n_dp)

            @pl.when(to < owners)
            def _():
                copy = pltpu.make_async_remote_copy(
                    src_ref=src.at[to],
                    dst_ref=land.at[d],
                    send_sem=send.at[to],
                    recv_sem=recv.at[d],
                    device_id={"dp": to},
                    device_id_type=MESH,
                )
                if start:
                    copy.start()
                else:
                    copy.wait_send()

    def wait_a(src, land, send, recv):
        for r in range(1, n_dp):
            come = lax.rem(d + r, n_dp)
            pltpu.make_async_remote_copy(
                src_ref=src.at[0],
                dst_ref=land.at[come],
                send_sem=send.at[0],
                recv_sem=recv.at[come],
                device_id={"dp": come},
                device_id_type=MESH,
            ).wait_recv()

    def phase_b(land, send, recv, start):
        for r in range(1, n_sp):
            to = lax.rem(s + r, n_sp)
            copy = pltpu.make_async_remote_copy(
                src_ref=land.at[s],
                dst_ref=land.at[s],
                send_sem=send.at[to],
                recv_sem=recv.at[s],
                device_id={"space": to},
                device_id_type=MESH,
            )
            if start:
                copy.start()
            else:
                copy.wait_send()

    def wait_b(land, send, recv):
        for r in range(1, n_sp):
            come = lax.rem(s + r, n_sp)
            pltpu.make_async_remote_copy(
                src_ref=land.at[come],
                dst_ref=land.at[come],
                send_sem=send.at[come],
                recv_sem=recv.at[come],
                device_id={"space": come},
                device_id_type=MESH,
            ).wait_recv()

    def phase_c(land, send, recv, start):
        for r in range(1, n_dp):
            to = lax.rem(d + r, n_dp)
            copy = pltpu.make_async_remote_copy(
                src_ref=land.at[d],
                dst_ref=land.at[d],
                send_sem=send.at[to],
                recv_sem=recv.at[d],
                device_id={"dp": to},
                device_id_type=MESH,
            )
            if start:
                copy.start()
            else:
                copy.wait_send()

    def wait_c(land, send, recv, owners):
        for r in range(1, n_dp):
            come = lax.rem(d + r, n_dp)

            @pl.when(come < owners)
            def _():
                pltpu.make_async_remote_copy(
                    src_ref=land.at[come],
                    dst_ref=land.at[come],
                    send_sem=send.at[come],
                    recv_sem=recv.at[come],
                    device_id={"dp": come},
                    device_id_type=MESH,
                ).wait_recv()

    own2 = -(-SLOTS // per2)
    per1 = -(-TILES // n_dp)
    own1 = -(-TILES // per1)

    phase_a(g2, r2, send_a2, recv_a2, own2, True)

    for pz in range(2):
        window_layer(win3, 1 + pz, lambda j, pz=pz: delta2[pz, j], 64, None)

    def back_window(qz, qy, a0, a1):
        return win3[qz + a0 : qz + a1, qy : qy + 3].reshape((a1 - a0) * 768, LANES)

    backs = []
    for qz in range(2):
        for qy in range(2):
            own = back_window(qz, qy, 1 - qz, 3 - qz)
            backs.append(dot(w2f[:, 768 * (1 - qz) : 768 * (3 - qz)], own))
    for copy in d_copies:
        copy.wait()
    grad1 = None
    sum1 = None
    for qz in range(2):
        keep = has_right if qz else has_left
        window_layer(win3, 3 * qz, lambda j, qz=qz: halo_d[qz, j], 64, keep)
        for qy in range(2):
            at = 2 * qz
            back = backs[2 * qz + qy] + dot(
                w2f[:, 768 * at : 768 * at + 768], back_window(qz, qy, at, at + 1)
            )
            back = back * 0.125
            for qx in range(2):
                q = 4 * qz + 2 * qy + qx
                one = back[32 * qx : 32 * qx + 32]
                delta1 = (one[None] * slope(act1[q])).astype(BF).reshape(256, LANES)
                term = dot_nt(delta1, first_window(q))
                part = dot_nt(ones[0:16], delta1)
                grad1 = term if grad1 is None else grad1 + term
                sum1 = part if sum1 is None else sum1 + part
    fold = grad1[0:32]
    for p in range(1, 8):
        by = 4 * (16 * (p // 4) + 4 * ((p // 2) % 2) + p % 2)
        fold = fold + pltpu.roll(grad1[32 * p : 32 * p + 32], LANES - by, 1)
    for t in range(8):
        rt, lt = t // 2, t % 2
        g1[t // per1, t % per1] = fold[8 * rt : 8 * rt + 8, 128 * lt : 128 * lt + 128]
    bias = sum1[0:8, 0:128] + sum1[0:8, 128:256]
    bias = bias + pltpu.roll(bias, 64, 1)
    bias = bias + pltpu.roll(bias, 96, 1)
    g1[8 // per1, 8 % per1] = bias
    for extra in range(TILES, per1 * own1):
        g1[extra // per1, extra % per1] = jnp.zeros((8, 128), F32)

    phase_a(g1, r1, send_a1, recv_a1, own1, True)

    sets = (
        (g2, r2, s2, f2, send_a2, recv_a2, send_b2, recv_b2, send_c2, recv_c2, own2),
        (g1, r1, s1, f1, send_a1, recv_a1, send_b1, recv_b1, send_c1, recv_c1, own1),
    )
    for g, r, sp, fin, sa, ra, sb, rb, sc, rc, own in sets:

        @pl.when(d < own)
        def _(g=g, r=r, sp=sp, sa=sa, ra=ra, sb=sb, rb=rb):
            r[d] = g[d]
            wait_a(g, r, sa, ra)
            total = r[0]
            for j in range(1, n_dp):
                total = total + r[j]
            sp[s] = total
            phase_b(sp, sb, rb, True)

    for g, r, sp, fin, sa, ra, sb, rb, sc, rc, own in sets:

        @pl.when(d < own)
        def _(sp=sp, fin=fin, sb=sb, rb=rb, sc=sc, rc=rc):
            wait_b(sp, sb, rb)
            total = sp[0]
            for j in range(1, n_sp):
                total = total + sp[j]
            fin[d] = total
            phase_c(fin, sc, rc, True)

    wait_c(f2, send_c2, recv_c2, own2)
    for k in range(27):
        both = f2[k // per2, k % per2]
        gw2_out[k, 0:16] = both[:, 0:64]
        gw2_out[k, 16:32] = pltpu.roll(both, 64, 1)[:, 0:64]
    gb2_out[...] = f2[27 // per2, 27 % per2][0:1, 0:64]
    wait_c(f1, send_c1, recv_c1, own1)
    rows = []
    for rt in range(4):
        rows.append(
            jnp.concatenate(
                [f1[(2 * rt + lt) // per1, (2 * rt + lt) % per1] for lt in range(2)], axis=1
            )
        )
    rows = jnp.concatenate(rows + [jnp.zeros((96, LANES), F32)], axis=0).T
    for k in range(27):
        at = 4 * (16 * (k // 9) + 4 * ((k // 3) % 3) + k % 3)
        gw1_out[k] = rows[at : at + 4, 0:32]
    gb1_out[...] = f1[8 // per1, 8 % per1][0:1, 0:32]

    for g, r, sp, fin, sa, ra, sb, rb, sc, rc, own in sets:
        phase_a(g, r, sa, ra, own, False)

        @pl.when(d < own)
        def _(sp=sp, fin=fin, sb=sb, rb=rb, sc=sc, rc=rc):
            phase_b(sp, sb, rb, False)
            phase_c(fin, sc, rc, False)


def solution(mesh):
    n_dp, n_sp = mesh.shape["dp"], mesh.shape["space"]
    per2 = -(-SLOTS // n_dp)
    per1 = -(-TILES // n_dp)
    vm = pl.BlockSpec(memory_space=pltpu.VMEM)

    def body(volume, w_first, b_first, w_second, b_second, cotangent):
        outs = pl.pallas_call(
            functools.partial(kernel, n_dp, n_sp),
            out_shape=(
                jax.ShapeDtypeStruct((64, LANES), BF),
                jax.ShapeDtypeStruct((27, 4, 32), F32),
                jax.ShapeDtypeStruct((1, 32), F32),
                jax.ShapeDtypeStruct((27, 32, 64), F32),
                jax.ShapeDtypeStruct((1, 64), F32),
            ),
            in_specs=[vm] * 6,
            out_specs=(vm,) * 5,
            scratch_shapes=[
                pltpu.VMEM((128, 6 * LANES), BF),
                pltpu.VMEM((2, 4, 32, 128), BF),
                pltpu.VMEM((2, 6, 6, 16, LANES), BF),
                pltpu.VMEM((256, 128), F32),
                pltpu.VMEM((256, 256), BF),
                pltpu.VMEM((128, 1152), BF),
                pltpu.VMEM((64, 2304), BF),
                pltpu.VMEM((8, 8, 32, LANES), F32),
                pltpu.VMEM((2, 4, 32, LANES), BF),
                pltpu.VMEM((2, 4, 32, LANES), BF),
                pltpu.VMEM((4, 4, 128, LANES), BF),
                pltpu.VMEM((2, 4, 64, LANES), BF),
                pltpu.VMEM((2, 4, 64, LANES), BF),
                pltpu.VMEM((4, 4, 256, LANES), BF),
                pltpu.VMEM((4, 128, LANES), F32),
                pltpu.VMEM((n_dp, per2, 16, 128), F32),
                pltpu.VMEM((n_dp, per2, 16, 128), F32),
                pltpu.VMEM((n_sp, per2, 16, 128), F32),
                pltpu.VMEM((n_dp, per2, 16, 128), F32),
                pltpu.VMEM((n_dp, per1, 8, 128), F32),
                pltpu.VMEM((n_dp, per1, 8, 128), F32),
                pltpu.VMEM((n_sp, per1, 8, 128), F32),
                pltpu.VMEM((n_dp, per1, 8, 128), F32),
                pltpu.SemaphoreType.DMA((6,)),
                pltpu.SemaphoreType.DMA((6,)),
            ]
            + [pltpu.SemaphoreType.DMA((n,)) for n in (n_dp, n_dp, n_sp, n_sp, n_dp, n_dp) * 2],
            compiler_params=pltpu.CompilerParams(collective_id=0, has_side_effects=True),
        )(
            volume.reshape(4, 4, 32, 128),
            w_first.transpose(0, 2, 1),
            b_first.reshape(1, 32),
            w_second.transpose(0, 2, 1),
            b_second.reshape(1, 64),
            cotangent.reshape(64, LANES),
        )
        top, gw1, gb1, gw2, gb2 = outs
        return (
            top.reshape(1, 64, 1, LANES),
            gw1.transpose(0, 2, 1),
            gb1.reshape(32),
            gw2.transpose(0, 2, 1),
            gb2.reshape(64),
        )

    in_specs = (
        P("dp", None, "space", None, None),
        P(),
        P(),
        P(),
        P(),
        P("dp", None, "space", None),
    )
    out_specs = (P("dp", None, "space", None), P(), P(), P(), P())
    return jax.shard_map(body, mesh=mesh, in_specs=in_specs, out_specs=out_specs, check_vma=False)
```

```python
import functools

import jax
import jax.numpy as jnp
from jax import lax
from jax.experimental import pallas as pl
from jax.experimental.pallas import tpu as pltpu
from jax.sharding import PartitionSpec as P

MESH = pl.DeviceIdType.MESH
BF = jnp.bfloat16
F32 = jnp.float32

LANES = 256
COLS = 32
SLOTS = 28
TILES = 8


def dot(a, b):
    return jnp.dot(a, b, preferred_element_type=F32)


def dot_nt(a, b):
    return lax.dot_general(a, b, (((1,), (1,)), ((), ())), preferred_element_type=F32)


def lane_of(shape):
    return lax.broadcasted_iota(jnp.int32, shape, len(shape) - 1)


def shift_x(v, step):
    lane = lane_of(v.shape)
    moved = pltpu.roll(v, step % LANES, 1)
    edge = 0 if step == 1 else COLS - 1
    return jnp.where(lane % COLS == edge, 0.0, moved)


def shift_y(v, step):
    lane = lane_of(v.shape)
    moved = pltpu.roll(v, (step * COLS) % LANES, 1)
    gone = lane < COLS if step == 1 else lane >= LANES - COLS
    return jnp.where(gone, 0.0, moved)


def leaky(v):
    return jnp.where(v > 0, v, 0.3 * v)


def slope(v):
    return jnp.where(v > 0, 1.0, 0.3)


def column(row):
    n = row.shape[1]
    r = lax.broadcasted_iota(jnp.int32, (n, n), 0)
    c = lax.broadcasted_iota(jnp.int32, (n, n), 1)
    return jnp.sum(jnp.where(r == c, jnp.broadcast_to(row, (n, n)), 0.0), axis=1, keepdims=True)


def window_layer(out, layer, raw, chans, keep):
    wide = []
    for qy in range(2):
        even = raw(2 * qy).astype(F32)
        odd = raw(2 * qy + 1).astype(F32)
        if keep is not None:
            even = jnp.where(keep, even, 0.0)
            odd = jnp.where(keep, odd, 0.0)
        wide.append(jnp.concatenate([shift_x(odd, 1), even, odd, shift_x(even, -1)], axis=0))
    out[layer, 0] = shift_y(wide[1], 1).astype(BF)
    out[layer, 1] = wide[0].astype(BF)
    out[layer, 2] = wide[1].astype(BF)
    out[layer, 3] = shift_y(wide[0], -1).astype(BF)


def kernel(
    n_dp,
    n_sp,
    vol_h,
    w1_h,
    b1_h,
    w2_h,
    b2_h,
    cot_h,
    top_out,
    f1,
    f2,
    vol,
    w1t,
    b1,
    w2t,
    b2,
    cot,
    pick,
    halo_v,
    ext,
    base_w,
    w1p,
    w2p,
    w2f,
    act1,
    pooled,
    halo_p,
    win2,
    delta2,
    give,
    halo_d,
    win3,
    acc,
    g2,
    r2,
    s2,
    t2,
    g1,
    r1,
    s1,
    t1,
    local_sem,
    halo_send,
    halo_recv,
    send_a2,
    recv_a2,
    send_b2,
    recv_b2,
    send_c2,
    recv_c2,
    send_a1,
    recv_a1,
    send_b1,
    recv_b1,
    send_c1,
    recv_c1,
):
    d = lax.axis_index("dp")
    s = lax.axis_index("space")
    left = lax.rem(s + n_sp - 1, n_sp)
    right = lax.rem(s + 1, n_sp)
    has_left = s > 0
    has_right = s < n_sp - 1

    n_g = n_dp // 2
    n_h = 2 * n_sp
    half, g = d // n_g, lax.rem(d, n_g)
    h = half * n_sp + s

    barrier = pltpu.get_barrier_semaphore()
    for r in range(1, n_sp):
        pl.semaphore_signal(
            barrier, inc=1, device_id={"space": lax.rem(s + r, n_sp)}, device_id_type=MESH
        )
    for r in range(1, n_dp):
        pl.semaphore_signal(
            barrier, inc=1, device_id={"dp": lax.rem(d + r, n_dp)}, device_id_type=MESH
        )
    for r in range(1, n_sp):
        pl.semaphore_signal(
            barrier,
            inc=1,
            device_id={"dp": (1 - half) * n_g + g, "space": lax.rem(s + r, n_sp)},
            device_id_type=MESH,
        )
    loads = [
        pltpu.make_async_copy(src, dst, local_sem.at[n])
        for n, (src, dst) in enumerate(
            ((vol_h, vol), (w1_h, w1t), (w2_h, w2t), (b1_h, b1), (b2_h, b2), (cot_h, cot))
        )
    ]
    for copy in loads:
        copy.start()

    for f in range(6):
        r = lax.broadcasted_iota(jnp.int32, (128, LANES), 0)
        c = lane_of((128, LANES)) % COLS
        pick[:, f * LANES : (f + 1) * LANES] = jnp.where(r == 4 * c + f - 1, 1.0, 0.0).astype(BF)
    row = lax.broadcasted_iota(jnp.int32, (64, 512), 0)
    col = lax.broadcasted_iota(jnp.int32, (64, 512), 1)
    gather = jnp.where(
        (row // 16 == col % 4) & ((row % 16) // 4 == col // 128) & (row % 4 == (col % 128) // 32),
        1.0,
        0.0,
    ).astype(BF)
    own_y = (lax.broadcasted_iota(jnp.int32, (128, LANES), 0) % 32) // 4 == lane_of(
        (128, LANES)
    ) // COLS

    def volume_layer(layer, plane):
        parts = []
        for f in range(6):
            spread = dot(plane, pick[:, f * LANES : (f + 1) * LANES])
            parts.append(jnp.where(own_y, spread, 0.0).astype(BF))
        for qx in range(2):
            cells = dot(gather, jnp.concatenate(parts[2 * qx : 2 * qx + 4], axis=0))
            ext[qx, layer, 0] = shift_y(cells[48:64], 1).astype(BF)
            for fy in range(4):
                ext[qx, layer, fy + 1] = cells[16 * fy : 16 * fy + 16].astype(BF)
            ext[qx, layer, 5] = shift_y(cells[0:16], -1).astype(BF)

    def halo_copy(src, dst, sem, to):
        return pltpu.make_async_remote_copy(
            src_ref=src,
            dst_ref=dst,
            send_sem=halo_send.at[sem],
            recv_sem=halo_recv.at[sem],
            device_id={"space": to},
            device_id_type=MESH,
        )

    loads[0].wait()
    pl.semaphore_wait(barrier, 2 * (n_sp - 1) + n_dp - 1)
    v_left = halo_copy(vol.at[:, 0], halo_v.at[1], 0, left)
    v_right = halo_copy(vol.at[:, 3], halo_v.at[0], 1, right)
    v_left.start()
    v_right.start()

    for z in range(4):
        volume_layer(z + 1, vol[:, z].reshape(128, 128))

    for copy in loads[1:]:
        copy.wait()
    base_w[...] = jnp.zeros_like(base_w)
    for k in range(27):
        at = 4 * (16 * (k // 9) + 4 * ((k // 3) % 3) + k % 3)
        base_w[at : at + 4, 0:32] = w1t[k].astype(F32)
    base = base_w[...].T[0:32]
    for p in range(8):
        by = 4 * (16 * (p // 4) + 4 * ((p // 2) % 2) + p % 2)
        w1p[32 * p : 32 * p + 32] = (pltpu.roll(base, by, 1) if by else base).astype(BF)
    none = jnp.zeros((32, 64), F32)
    for ac in range(9):
        taps = [w2t[3 * ac + e].astype(F32) for e in range(3)]
        blocks = [
            jnp.concatenate([taps[w] if w < 3 else none, taps[w - 1] if w > 0 else none], axis=1)
            for w in range(4)
        ]
        w2p[:, 128 * ac : 128 * ac + 128] = jnp.concatenate(blocks, axis=0).T.astype(BF)
        down, at = 64 * (2 - ac // 3), 256 * (2 - ac % 3)
        w2f[down : down + 32, at : at + 256] = jnp.concatenate(
            [taps[2], taps[1], taps[0], none], axis=1
        ).astype(BF)
        w2f[down + 32 : down + 64, at : at + 256] = jnp.concatenate(
            [none, taps[2], taps[1], taps[0]], axis=1
        ).astype(BF)
    b1c = column(b1[...])
    b2c = column(b2[...])

    v_left.wait_recv()
    v_right.wait_recv()
    for side, keep in ((0, has_left), (1, has_right)):
        plane = halo_v[side].reshape(128, 128).astype(F32)
        volume_layer(5 * side, jnp.where(keep, plane, 0.0).astype(BF))

    def first_window(q):
        qz, qy, qx = q // 4, (q // 2) % 2, q % 2
        return ext[qx, 2 * qz : 2 * qz + 4, 2 * qy : 2 * qy + 4].reshape(256, LANES)

    p_copies = []
    for qz in range(2):
        for qq in range(4):
            q = 4 * qz + qq
            act = dot(w1p[...], first_window(q)).reshape(8, 32, LANES) + b1c[None]
            act1[q] = act
            pooled[qz, qq] = (jnp.sum(leaky(act), axis=0) * 0.125).astype(BF)
        copy = halo_copy(pooled.at[qz], halo_p.at[1 - qz], 2 + qz, right if qz else left)
        copy.start()
        p_copies.append(copy)

    for qz in range(2):
        window_layer(win2, 1 + qz, lambda j, qz=qz: pooled[qz, j], 32, None)

    def second_window(pz, py, a0, a1):
        return win2[pz + a0 : pz + a1, py : py + 3].reshape((a1 - a0) * 384, LANES)

    for pz in range(2):
        for py in range(2):
            own = second_window(pz, py, 1 - pz, 3 - pz)
            acc[2 * pz + py] = dot(w2p[:, 384 * (1 - pz) : 384 * (3 - pz)], own)
    grad_top = cot[...].astype(F32) * 0.125
    top = jnp.zeros((64, LANES), F32)
    backs = [[None, None], [None, None]]
    d_copies = []
    for pz in range(2):
        p_copies[1 - pz].wait_recv()
        keep = has_right if pz else has_left
        window_layer(win2, 3 * pz, lambda j, pz=pz: halo_p[pz, j], 32, keep)
        for py in range(2):
            at = 2 * pz
            act = acc[2 * pz + py] + dot(
                w2p[:, 384 * at : 384 * at + 384], second_window(pz, py, at, at + 1)
            )
            for px in range(2):
                one = act[64 * px : 64 * px + 64] + b2c
                top = top + leaky(one)
                delta2[pz, 2 * py + px] = (grad_top * slope(one)).astype(BF)
        window_layer(win3, pz, lambda j, pz=pz: delta2[pz, j], 64, None)
        for qy in range(2):
            three = dot(w2f[...], win3[pz, qy : qy + 3].reshape(768, LANES))
            for a in range(3):
                qz, part = 1 + pz - a, three[64 * a : 64 * a + 64]
                if 0 <= qz < 2:
                    there = backs[qz][qy]
                    backs[qz][qy] = part if there is None else there + part
                else:
                    give[pz, qy] = part.astype(BF)
        copy = halo_copy(give.at[pz], halo_d.at[1 - pz], 4 + pz, right if pz else left)
        copy.start()
        d_copies.append(copy)
    top_out[...] = (top * 0.125).astype(BF)

    ones = jnp.ones((16, LANES), BF)
    grad = None
    sums = None
    for pz in range(2):
        for py in range(2):
            there = delta2[pz, 2 * py : 2 * py + 2].reshape(128, LANES)
            term = dot_nt(second_window(pz, py, 0, 3), there)
            part = dot_nt(ones, there)
            grad = term if grad is None else grad + term
            sums = part if sums is None else sums + part
    low = lane_of((16, 128)) < 64
    per2 = -(-SLOTS // n_dp)
    for k in range(27):
        at = 128 * (k // 3) + 32 * (k % 3)
        here, after = grad[at : at + 32], grad[at + 32 : at + 64]
        first = here[0:16] + pltpu.roll(after[0:16], 64, 1)
        second = pltpu.roll(here[16:32], 64, 1) + after[16:32]
        g2[k // per2, k % per2] = jnp.where(low, first, second)
    g2[27 // per2, 27 % per2] = sums + pltpu.roll(sums, 64, 1)
    for extra in range(SLOTS, per2 * (-(-SLOTS // per2))):
        g2[extra // per2, extra % per2] = jnp.zeros((16, 128), F32)

    def to_dp(j):
        return {"dp": j}

    def to_space(j):
        return {"space": j}

    def to_g(j):
        return {"dp": half * n_g + j}

    def to_h(j):
        return {"dp": (j // n_sp) * n_g + g, "space": lax.rem(j, n_sp)}

    def send_all(me, n, owners, where, src, dst, send, recv, start):
        for r in range(1, n):
            to = lax.rem(me + r, n)

            def one():
                copy = pltpu.make_async_remote_copy(
                    src_ref=src(to),
                    dst_ref=dst,
                    send_sem=send.at[to],
                    recv_sem=recv.at[me],
                    device_id=where(to),
                    device_id_type=MESH,
                )
                if start:
                    copy.start()
                else:
                    copy.wait_send()

            if owners < n:
                pl.when(to < owners)(one)
            else:
                one()

    def take_all(me, n, owners, where, land, send, recv):
        for r in range(1, n):
            come = lax.rem(me + r, n)

            def one():
                pltpu.make_async_remote_copy(
                    src_ref=land.at[come],
                    dst_ref=land.at[come],
                    send_sem=send.at[come],
                    recv_sem=recv.at[come],
                    device_id=where(come),
                    device_id_type=MESH,
                ).wait_recv()

            if owners < n:
                pl.when(come < owners)(one)
            else:
                one()

    own2 = -(-SLOTS // per2)
    per1 = TILES // n_g

    def start_a2(start):
        send_all(d, n_dp, own2, to_dp, lambda to: g2.at[to], r2.at[d], send_a2, recv_a2, start)

    def start_b2(start):
        send_all(s, n_sp, n_sp, to_space, lambda to: s2.at[s], s2.at[s], send_b2, recv_b2, start)

    def start_c2(start):
        send_all(d, n_dp, n_dp, to_dp, lambda to: t2, f2.at[d], send_c2, recv_c2, start)

    def start_a1(start):
        send_all(g, n_g, n_g, to_g, lambda to: g1.at[to], r1.at[g], send_a1, recv_a1, start)

    def start_b1(start):
        send_all(h, n_h, n_h, to_h, lambda to: s1.at[h], s1.at[h], send_b1, recv_b1, start)

    def start_c1(start):
        send_all(g, n_g, n_g, to_g, lambda to: t1, f1.at[g], send_c1, recv_c1, start)

    def added(ref, n):
        total = ref[0]
        for j in range(1, n):
            total = total + ref[j]
        return total

    start_a2(True)

    grad1 = None
    sum1 = None
    for qz in range(2):
        keep = has_right if qz else has_left
        d_copies[1 - qz].wait_recv()
        for qy in range(2):
            back = backs[qz][qy] + jnp.where(keep, halo_d[qz, qy].astype(F32), 0.0)
            back = back * 0.125
            for qx in range(2):
                q = 4 * qz + 2 * qy + qx
                one = back[32 * qx : 32 * qx + 32]
                delta1 = (one[None] * slope(act1[q])).astype(BF).reshape(256, LANES)
                term = dot_nt(delta1, first_window(q))
                part = dot_nt(ones[0:16], delta1)
                grad1 = term if grad1 is None else grad1 + term
                sum1 = part if sum1 is None else sum1 + part
    fold = grad1[0:32]
    for p in range(1, 8):
        by = 4 * (16 * (p // 4) + 4 * ((p // 2) % 2) + p % 2)
        fold = fold + pltpu.roll(grad1[32 * p : 32 * p + 32], LANES - by, 1)
    bias = sum1[0:8, 0:128] + sum1[0:8, 128:256]
    bias = bias + pltpu.roll(bias, 64, 1)
    bias = bias + pltpu.roll(bias, 96, 1)
    fold = jnp.where(lane_of((32, LANES)) == LANES - 1, column(bias[0:1, 0:32]), fold)
    for t in range(8):
        rt, lt = t // 2, t % 2
        g1[t // per1, t % per1] = fold[8 * rt : 8 * rt + 8, 128 * lt : 128 * lt + 128]

    start_a1(True)

    @pl.when(d < own2)
    def _():
        r2[d] = g2[d]
        take_all(d, n_dp, n_dp, to_dp, r2, send_a2, recv_a2)
        s2[s] = added(r2, n_dp)
        start_b2(True)

    r1[g] = g1[g]
    take_all(g, n_g, n_g, to_g, r1, send_a1, recv_a1)
    s1[h] = added(r1, n_g)
    start_b1(True)

    mine2 = pltpu.make_async_copy(t2, f2.at[d], local_sem.at[0])
    mine1 = pltpu.make_async_copy(t1, f1.at[g], local_sem.at[1])

    @pl.when(d < own2)
    def _():
        take_all(s, n_sp, n_sp, to_space, s2, send_b2, recv_b2)
        t2[...] = added(s2, n_sp).astype(BF)
        start_c2(True)
        mine2.start()

    take_all(h, n_h, n_h, to_h, s1, send_b1, recv_b1)
    t1[...] = added(s1, n_h)
    start_c1(True)
    mine1.start()

    for copy in [v_left, v_right] + p_copies + d_copies:
        copy.wait_send()
    start_a2(False)
    start_a1(False)
    start_b1(False)

    @pl.when(d < own2)
    def _():
        start_b2(False)
        mine2.wait()
        start_c2(False)

    mine1.wait()
    start_c1(False)
    take_all(d, n_dp, own2, to_dp, f2, send_c2, recv_c2)
    take_all(g, n_g, n_g, to_g, f1, send_c1, recv_c1)


def finish(per2, per1, top, f1, f2, top_out, gw1_out, gb1_out, gw2_out, gb2_out):
    top_out[...] = top[...]
    for k in range(27):
        both = f2[k // per2, k % per2].astype(F32)
        gw2_out[k, 0:16] = both[:, 0:64]
        gw2_out[k, 16:32] = pltpu.roll(both, 64, 1)[:, 0:64]
    gb2_out[...] = f2[27 // per2, 27 % per2].astype(F32)[0:1, 0:64]
    rows = []
    for rt in range(4):
        tiles = [f1[(2 * rt + lt) // per1, (2 * rt + lt) % per1] for lt in range(2)]
        rows.append(jnp.concatenate(tiles, axis=1))
    rows = jnp.concatenate(rows + [jnp.zeros((96, LANES), F32)], axis=0).T
    for k in range(27):
        at = 4 * (16 * (k // 9) + 4 * ((k // 3) % 3) + k % 3)
        gw1_out[k] = rows[at : at + 4, 0:32]
    gb1_out[...] = rows[LANES - 1 : LANES, 0:32]


def solution(mesh):
    n_dp, n_sp = mesh.shape["dp"], mesh.shape["space"]
    per2 = -(-SLOTS // n_dp)
    own2 = -(-SLOTS // per2)
    n_g, n_h = n_dp // 2, 2 * n_sp
    per1 = TILES // n_g
    vm = pl.BlockSpec(memory_space=pltpu.VMEM)
    anywhere = pl.BlockSpec(memory_space=pl.ANY)

    def body(volume, w_first, b_first, w_second, b_second, cotangent):
        parts = pl.pallas_call(
            functools.partial(kernel, n_dp, n_sp),
            out_shape=(
                jax.ShapeDtypeStruct((64, LANES), BF),
                jax.ShapeDtypeStruct((n_g, per1, 8, 128), F32),
                jax.ShapeDtypeStruct((own2, per2, 16, 128), BF),
            ),
            in_specs=[anywhere] * 6,
            out_specs=(vm, anywhere, anywhere),
            scratch_shapes=[
                pltpu.VMEM((4, 4, 32, 128), BF),
                pltpu.VMEM((27, 4, 32), BF),
                pltpu.VMEM((1, 32), F32),
                pltpu.VMEM((27, 32, 64), BF),
                pltpu.VMEM((1, 64), F32),
                pltpu.VMEM((64, LANES), BF),
                pltpu.VMEM((128, 6 * LANES), BF),
                pltpu.VMEM((2, 4, 32, 128), BF),
                pltpu.VMEM((2, 6, 6, 16, LANES), BF),
                pltpu.VMEM((256, 128), F32),
                pltpu.VMEM((256, 256), BF),
                pltpu.VMEM((128, 1152), BF),
                pltpu.VMEM((192, 768), BF),
                pltpu.VMEM((8, 8, 32, LANES), F32),
                pltpu.VMEM((2, 4, 32, LANES), BF),
                pltpu.VMEM((2, 4, 32, LANES), BF),
                pltpu.VMEM((4, 4, 128, LANES), BF),
                pltpu.VMEM((2, 4, 64, LANES), BF),
                pltpu.VMEM((2, 2, 64, LANES), BF),
                pltpu.VMEM((2, 2, 64, LANES), BF),
                pltpu.VMEM((2, 4, 256, LANES), BF),
                pltpu.VMEM((4, 128, LANES), F32),
                pltpu.VMEM((n_dp, per2, 16, 128), F32),
                pltpu.VMEM((n_dp, per2, 16, 128), F32),
                pltpu.VMEM((n_sp, per2, 16, 128), F32),
                pltpu.VMEM((per2, 16, 128), BF),
                pltpu.VMEM((n_g, per1, 8, 128), F32),
                pltpu.VMEM((n_g, per1, 8, 128), F32),
                pltpu.VMEM((n_h, per1, 8, 128), F32),
                pltpu.VMEM((per1, 8, 128), F32),
            ]
            + [
                pltpu.SemaphoreType.DMA((n,))
                for n in (6, 6, 6)
                + (n_dp, n_dp, n_sp, n_sp, n_dp, n_dp)
                + (n_g, n_g, n_h, n_h, n_g, n_g)
            ],
            compiler_params=pltpu.CompilerParams(collective_id=0, has_side_effects=True),
            name="step",
        )(
            volume.reshape(4, 4, 32, 128),
            w_first.transpose(0, 2, 1),
            b_first.reshape(1, 32),
            w_second.transpose(0, 2, 1),
            b_second.reshape(1, 64),
            cotangent.reshape(64, LANES),
        )
        top, gw1, gb1, gw2, gb2 = pl.pallas_call(
            functools.partial(finish, per2, per1),
            out_shape=(
                jax.ShapeDtypeStruct((64, LANES), BF),
                jax.ShapeDtypeStruct((27, 4, 32), F32),
                jax.ShapeDtypeStruct((1, 32), F32),
                jax.ShapeDtypeStruct((27, 32, 64), F32),
                jax.ShapeDtypeStruct((1, 64), F32),
            ),
            in_specs=[vm] * 3,
            out_specs=(vm,) * 5,
            name="finish",
        )(*parts)
        return (
            top.reshape(1, 64, 1, LANES),
            gw1.transpose(0, 2, 1),
            gb1.reshape(32),
            gw2.transpose(0, 2, 1),
            gb2.reshape(64),
        )

    in_specs = (
        P("dp", None, "space", None, None),
        P(),
        P(),
        P(),
        P(),
        P("dp", None, "space", None),
    )
    out_specs = (P("dp", None, "space", None), P(), P(), P(), P())
    return jax.shard_map(body, mesh=mesh, in_specs=in_specs, out_specs=out_specs, check_vma=False)
```

```python
import functools

import jax
import jax.numpy as jnp
from jax import lax
from jax.experimental import pallas as pl
from jax.experimental.pallas import tpu as pltpu
from jax.sharding import PartitionSpec as P

MESH = pl.DeviceIdType.MESH
BF = jnp.bfloat16
F32 = jnp.float32

LANES = 256
COLS = 32
SLOTS = 28
TILES = 8


def dot(a, b):
    return jnp.dot(a, b, preferred_element_type=F32)


def dot_nt(a, b):
    return lax.dot_general(a, b, (((1,), (1,)), ((), ())), preferred_element_type=F32)


def lane_of(shape):
    return lax.broadcasted_iota(jnp.int32, shape, len(shape) - 1)


def shift_x(v, step):
    lane = lane_of(v.shape)
    moved = pltpu.roll(v, step % LANES, 1)
    edge = 0 if step == 1 else COLS - 1
    return jnp.where(lane % COLS == edge, 0.0, moved)


def shift_y(v, step):
    lane = lane_of(v.shape)
    moved = pltpu.roll(v, (step * COLS) % LANES, 1)
    gone = lane < COLS if step == 1 else lane >= LANES - COLS
    return jnp.where(gone, 0.0, moved)


def leaky(v):
    return jnp.maximum(v, 0.3 * v)


def slope(v):
    return jnp.where(v > 0, 1.0, 0.3)


def column(row):
    n = row.shape[1]
    r = lax.broadcasted_iota(jnp.int32, (n, n), 0)
    c = lax.broadcasted_iota(jnp.int32, (n, n), 1)
    return jnp.sum(jnp.where(r == c, jnp.broadcast_to(row, (n, n)), 0.0), axis=1, keepdims=True)


def window_layer(out, layer, raw, chans, keep):
    wide = []
    for qy in range(2):
        even = raw(2 * qy).astype(F32)
        odd = raw(2 * qy + 1).astype(F32)
        if keep is not None:
            even = jnp.where(keep, even, 0.0)
            odd = jnp.where(keep, odd, 0.0)
        wide.append(jnp.concatenate([shift_x(odd, 1), even, odd, shift_x(even, -1)], axis=0))
    out[layer, 0] = shift_y(wide[1], 1).astype(BF)
    out[layer, 1] = wide[0].astype(BF)
    out[layer, 2] = wide[1].astype(BF)
    out[layer, 3] = shift_y(wide[0], -1).astype(BF)


def kernel(
    n_dp,
    n_sp,
    vol_h,
    w1_h,
    b1_h,
    w2_h,
    b2_h,
    cot_h,
    top_out,
    f1,
    f2,
    vol,
    w1t,
    b1,
    w2t,
    b2,
    cot,
    pick,
    halo_v,
    ext,
    base_w,
    w1p,
    w2p,
    w2f,
    act1,
    pooled,
    halo_p,
    win2,
    delta2,
    give,
    halo_d,
    win3,
    acc,
    d1,
    g2,
    r2,
    s2,
    t2,
    g1,
    r1,
    s1,
    t1,
    local_sem,
    send_sem,
    recv_sem,
):
    d = lax.axis_index("dp")
    s = lax.axis_index("space")
    left = lax.rem(s + n_sp - 1, n_sp)
    right = lax.rem(s + 1, n_sp)
    has_left = s > 0
    has_right = s < n_sp - 1

    n_g = n_dp // 2
    n_h = 2 * n_sp
    n_z, n_y = n_g // 2, n_sp // 2
    half, g = d // n_g, lax.rem(d, n_g)
    z, core = g // 2, lax.rem(g, 2)
    x_hi, y = s // n_y, lax.rem(s, n_y)
    h = half * n_sp + s

    def ring(step, n):
        return min(step, n - step)

    def peers(x_lo_too, z_too, space_too):
        found = []
        for dx in range(2 if x_lo_too else 1):
            for dz in range(n_z if z_too else 1):
                for dc in range(2 if z_too else 1):
                    for dh in range(2 if space_too else 1):
                        for dy in range(n_y if space_too else 1):
                            if dx + dz + dc + dh + dy == 0:
                                continue
                            hops = ring(dz, n_z) + ring(dy, n_y) + (1 if dx else 2 * dh)
                            found.append((hops, dx, dz, dc, dh, dy))
        found.sort(reverse=True)
        out = []
        for _, dx, dz, dc, dh, dy in found:
            half_to = lax.rem(half + dx, 2)
            g_to = lax.rem(z + dz, n_z) * 2 + lax.rem(core + dc, 2)
            s_to = lax.rem(x_hi + dh, 2) * n_y + lax.rem(y + dy, n_y)
            if space_too:
                at = half_to * n_sp + s_to if x_lo_too else s_to
            else:
                at = half_to * n_g + g_to if x_lo_too else g_to
            device = {}
            if x_lo_too or z_too:
                device["dp"] = half_to * n_g + g_to
            if space_too:
                device["space"] = s_to
            out.append((at, device))
        return out

    dp_peers = peers(True, True, False)
    g_peers = peers(False, True, False)
    h_peers = peers(True, False, True)
    s_peers = peers(False, False, True)

    barrier = pltpu.get_barrier_semaphore()
    for _, device in h_peers + dp_peers:
        pl.semaphore_signal(barrier, inc=1, device_id=device, device_id_type=MESH)
    loads = [
        pltpu.make_async_copy(src, dst, local_sem.at[n])
        for n, (src, dst) in enumerate(
            ((vol_h, vol), (w1_h, w1t), (w2_h, w2t), (b1_h, b1), (b2_h, b2), (cot_h, cot))
        )
    ]
    for copy in loads:
        copy.start()

    for f in range(6):
        r = lax.broadcasted_iota(jnp.int32, (128, LANES), 0)
        c = lane_of((128, LANES)) % COLS
        pick[:, f * LANES : (f + 1) * LANES] = jnp.where(r == 4 * c + f - 1, 1.0, 0.0).astype(BF)
    row = lax.broadcasted_iota(jnp.int32, (64, 512), 0)
    col = lax.broadcasted_iota(jnp.int32, (64, 512), 1)
    gather = jnp.where(
        (row // 16 == col % 4) & ((row % 16) // 4 == col // 128) & (row % 4 == (col % 128) // 32),
        1.0,
        0.0,
    ).astype(BF)
    own_y = (lax.broadcasted_iota(jnp.int32, (256, LANES), 0) % 32) // 4 == lane_of(
        (256, LANES)
    ) // COLS

    def volume_layers(layers, planes):
        both = jnp.concatenate(planes, axis=0)
        parts = []
        for f in range(6):
            spread = dot(both, pick[:, f * LANES : (f + 1) * LANES])
            parts.append(jnp.where(own_y, spread, 0.0).astype(BF))
        for n, layer in enumerate(layers):
            for qx in range(2):
                mine = [part[128 * n : 128 * n + 128] for part in parts[2 * qx : 2 * qx + 4]]
                cells = dot(gather, jnp.concatenate(mine, axis=0))
                ext[qx, layer, 0] = shift_y(cells[48:64], 1).astype(BF)
                for fy in range(4):
                    ext[qx, layer, fy + 1] = cells[16 * fy : 16 * fy + 16].astype(BF)
                ext[qx, layer, 5] = shift_y(cells[0:16], -1).astype(BF)

    def halo_copy(src, dst, sem, to):
        return pltpu.make_async_remote_copy(
            src_ref=src,
            dst_ref=dst,
            send_sem=send_sem.at[sem],
            recv_sem=recv_sem.at[sem],
            device_id={"space": to},
            device_id_type=MESH,
        )

    loads[0].wait()
    pl.semaphore_wait(barrier, n_h - 1 + n_dp - 1)
    v_left = halo_copy(vol.at[:, 0], halo_v.at[1], 0, left)
    v_right = halo_copy(vol.at[:, 3], halo_v.at[0], 1, right)
    v_left.start()
    v_right.start()

    for pair in (0, 2):
        volume_layers(
            (pair + 1, pair + 2), [vol[:, pair + n].reshape(128, 128) for n in range(2)]
        )

    for copy in loads[1:]:
        copy.wait()
    base_w[...] = jnp.zeros_like(base_w)
    for k in range(27):
        at = 4 * (16 * (k // 9) + 4 * ((k // 3) % 3) + k % 3)
        base_w[at : at + 4, 0:32] = w1t[k].astype(F32)
    base = base_w[...].T[0:32]
    for p in range(8):
        by = 4 * (16 * (p // 4) + 4 * ((p // 2) % 2) + p % 2)
        w1p[32 * p : 32 * p + 32] = (pltpu.roll(base, by, 1) if by else base).astype(BF)
    none = jnp.zeros((32, 64), F32)
    for ac in range(9):
        taps = [w2t[3 * ac + e].astype(F32) for e in range(3)]
        blocks = [
            jnp.concatenate([taps[w] if w < 3 else none, taps[w - 1] if w > 0 else none], axis=1)
            for w in range(4)
        ]
        w2p[:, 128 * ac : 128 * ac + 128] = jnp.concatenate(blocks, axis=0).T.astype(BF)
        down, at = 64 * (2 - ac // 3), 256 * (2 - ac % 3)
        w2f[down : down + 32, at : at + 256] = jnp.concatenate(
            [taps[2], taps[1], taps[0], none], axis=1
        ).astype(BF)
        w2f[down + 32 : down + 64, at : at + 256] = jnp.concatenate(
            [none, taps[2], taps[1], taps[0]], axis=1
        ).astype(BF)
    b1c = column(b1[...])
    b2c = column(b2[...])

    v_left.wait_recv()
    v_right.wait_recv()
    planes = []
    for side, keep in ((0, has_left), (1, has_right)):
        plane = halo_v[side].reshape(128, 128).astype(F32)
        planes.append(jnp.where(keep, plane, 0.0).astype(BF))
    volume_layers((0, 5), planes)

    def first_window(q):
        qz, qy, qx = q // 4, (q // 2) % 2, q % 2
        return ext[qx, 2 * qz : 2 * qz + 4, 2 * qy : 2 * qy + 4].reshape(256, LANES)

    for qy in range(2):
        for qz in range(2):
            for qx in range(2):
                q = 4 * qz + 2 * qy + qx
                act = dot(w1p[...], first_window(q)).reshape(8, 32, LANES) + b1c[None]
                act1[q] = act
                pooled[qz, 2 * qy + qx] = (jnp.sum(leaky(act), axis=0) * 0.125).astype(BF)
            rows = slice(2 * qy, 2 * qy + 2)
            halo_copy(
                pooled.at[qz, rows], halo_p.at[1 - qz, rows], 2 + qz, right if qz else left
            ).start()
    p_copies = [halo_copy(pooled.at[qz], halo_p.at[1 - qz], 2 + qz, left) for qz in range(2)]

    for qz in range(2):
        window_layer(win2, 1 + qz, lambda j, qz=qz: pooled[qz, j], 32, None)

    def second_window(pz, py, a0, a1):
        return win2[pz + a0 : pz + a1, py : py + 3].reshape((a1 - a0) * 384, LANES)

    for pz in range(2):
        for py in range(2):
            own = second_window(pz, py, 1 - pz, 3 - pz)
            acc[2 * pz + py] = dot(w2p[:, 384 * (1 - pz) : 384 * (3 - pz)], own)
    grad_top = cot[...].astype(F32) * 0.125
    top = jnp.zeros((64, LANES), F32)
    backs = [[None, None], [None, None]]
    for pz in range(2):
        p_copies[1 - pz].wait_recv()
    for pz in range(2):
        keep = has_right if pz else has_left
        window_layer(win2, 3 * pz, lambda j, pz=pz: halo_p[pz, j], 32, keep)
    for pz in range(2):
        for py in range(2):
            at = 2 * pz
            act = acc[2 * pz + py] + dot(
                w2p[:, 384 * at : 384 * at + 384], second_window(pz, py, at, at + 1)
            )
            for px in range(2):
                one = act[64 * px : 64 * px + 64] + b2c
                top = top + leaky(one)
                delta2[pz, 2 * py + px] = (grad_top * slope(one)).astype(BF)
    for pz in range(2):
        window_layer(win3, pz, lambda j, pz=pz: delta2[pz, j], 64, None)
    for qy in range(2):
        for pz in range(2):
            three = dot(w2f[...], win3[pz, qy : qy + 3].reshape(768, LANES))
            for a in range(3):
                qz, part = 1 + pz - a, three[64 * a : 64 * a + 64]
                if 0 <= qz < 2:
                    there = backs[qz][qy]
                    backs[qz][qy] = part if there is None else there + part
                else:
                    give[pz, qy] = part.astype(BF)
            halo_copy(
                give.at[pz, qy], halo_d.at[1 - pz, qy], 4 + pz, right if pz else left
            ).start()
    d_copies = [halo_copy(give.at[pz], halo_d.at[1 - pz], 4 + pz, left) for pz in range(2)]
    top_out[...] = (top * 0.125).astype(BF)

    both = [(pz, py) for pz in range(2) for py in range(2)]
    there = jnp.concatenate(
        [delta2[pz, 2 * py : 2 * py + 2].reshape(128, LANES) for pz, py in both], axis=1
    )
    grad = dot_nt(jnp.concatenate([second_window(*b, 0, 3) for b in both], axis=1), there)
    sums = dot_nt(jnp.ones((16, 4 * LANES), BF), there)
    low = lane_of((16, 128)) < 64
    per2 = -(-SLOTS // n_dp)
    for k in range(27):
        at = 128 * (k // 3) + 32 * (k % 3)
        here, after = grad[at : at + 32], grad[at + 32 : at + 64]
        first = here[0:16] + pltpu.roll(after[0:16], 64, 1)
        second = pltpu.roll(here[16:32], 64, 1) + after[16:32]
        g2[k // per2, k % per2] = jnp.where(low, first, second)
    g2[27 // per2, 27 % per2] = sums + pltpu.roll(sums, 64, 1)
    for extra in range(SLOTS, per2 * (-(-SLOTS // per2))):
        g2[extra // per2, extra % per2] = jnp.zeros((16, 128), F32)

    def send_all(me, others, src, dst, sem, owners=None):
        for to, device in others:

            def one():
                pltpu.make_async_remote_copy(
                    src_ref=src(to),
                    dst_ref=dst,
                    send_sem=send_sem.at[sem],
                    recv_sem=recv_sem.at[sem],
                    device_id=device,
                    device_id_type=MESH,
                ).start()

            if owners is None:
                one()
            else:
                pl.when(to < owners)(one)

    def all_of(ref, n, sem):
        return pltpu.make_async_remote_copy(
            src_ref=ref.at[0:n],
            dst_ref=ref.at[0:n],
            send_sem=send_sem.at[sem],
            recv_sem=recv_sem.at[sem],
            device_id={"space": right},
            device_id_type=MESH,
        )

    own2 = -(-SLOTS // per2)
    per1 = TILES // n_g

    is_owner = d < own2

    def added(ref, n):
        total = ref[0]
        for j in range(1, n):
            total = total + ref[j]
        return total

    send_all(d, dp_peers, lambda to: g2.at[to], r2.at[d], 6, own2)

    for q in range(8):
        act1[q] = jnp.where(act1[q] > 0, 0.125, 0.3 * 0.125)

    for qz in range(2):
        d_copies[1 - qz].wait_recv()
    for qz in range(2):
        keep = has_right if qz else has_left
        for qy in range(2):
            back = backs[qz][qy] + jnp.where(keep, halo_d[qz, qy].astype(F32), 0.0)
            for qx in range(2):
                q = 4 * qz + 2 * qy + qx
                one = back[32 * qx : 32 * qx + 32]
                d1[:, LANES * q : LANES * q + LANES] = (
                    (one[None] * act1[q]).astype(BF).reshape(256, LANES)
                )
    windows = jnp.concatenate([first_window(q) for q in range(8)], axis=1)
    grad1 = dot_nt(d1[...], windows)
    sum1 = dot_nt(d1[...], jnp.ones((128, 8 * LANES), BF))
    fold = grad1[0:32]
    bias = sum1[0:32]
    for p in range(1, 8):
        by = 4 * (16 * (p // 4) + 4 * ((p // 2) % 2) + p % 2)
        fold = fold + pltpu.roll(grad1[32 * p : 32 * p + 32], LANES - by, 1)
        bias = bias + sum1[32 * p : 32 * p + 32]
    fold = jnp.where(
        lane_of((32, LANES)) == LANES - 1, jnp.concatenate([bias, bias], axis=1), fold
    )
    for t in range(8):
        rt, lt = t // 2, t % 2
        g1[t // per1, t % per1] = fold[8 * rt : 8 * rt + 8, 128 * lt : 128 * lt + 128]

    send_all(g, g_peers, lambda to: g1.at[to], r1.at[g], 7)

    @pl.when(is_owner)
    def _():
        r2[d] = g2[d]
        all_of(r2, n_dp - 1, 6).wait_recv()
        s2[s] = added(r2, n_dp)
        send_all(s, s_peers, lambda to: s2.at[s], s2.at[s], 8)

    r1[g] = g1[g]
    all_of(r1, n_g - 1, 7).wait_recv()
    s1[h] = added(r1, n_g)
    send_all(h, h_peers, lambda to: s1.at[h], s1.at[h], 9)

    mine2 = pltpu.make_async_copy(t2, f2.at[d], local_sem.at[0])
    mine1 = pltpu.make_async_copy(t1, f1.at[g], local_sem.at[1])

    @pl.when(is_owner)
    def _():
        all_of(s2, n_sp - 1, 8).wait_recv()
        t2[...] = added(s2, n_sp).astype(BF)
        send_all(d, dp_peers, lambda to: t2, f2.at[d], 10)
        mine2.start()

    all_of(s1, n_h - 1, 9).wait_recv()
    t1[...] = added(s1, n_h)
    send_all(g, g_peers, lambda to: t1, f1.at[g], 11)
    mine1.start()

    for copy in [v_left, v_right] + p_copies + d_copies:
        copy.wait_send()
    all_of(g1, n_g - 1, 7).wait_send()
    all_of(s1, n_h - 1, 9).wait_send()

    @pl.when(is_owner)
    def _():
        all_of(g2, own2 - 1, 6).wait_send()
        all_of(s2, n_sp - 1, 8).wait_send()
        mine2.wait()
        all_of(f2, n_dp - 1, 10).wait_send()
        all_of(f2, own2 - 1, 10).wait_recv()

    @pl.when(jnp.logical_not(is_owner))
    def _():
        all_of(g2, own2, 6).wait_send()
        all_of(f2, own2, 10).wait_recv()

    mine1.wait()
    all_of(f1, n_g - 1, 11).wait_send()
    all_of(f1, n_g - 1, 11).wait_recv()


def finish(per2, per1, top, f1, f2, top_out, gw1_out, gb1_out, gw2_out, gb2_out):
    top_out[...] = top[...]
    for k in range(27):
        both = f2[k // per2, k % per2].astype(F32)
        gw2_out[k, 0:16] = both[:, 0:64]
        gw2_out[k, 16:32] = pltpu.roll(both, 64, 1)[:, 0:64]
    gb2_out[...] = f2[27 // per2, 27 % per2].astype(F32)[0:1, 0:64]
    rows = []
    for rt in range(4):
        tiles = [f1[(2 * rt + lt) // per1, (2 * rt + lt) % per1] for lt in range(2)]
        rows.append(jnp.concatenate(tiles, axis=1))
    rows = jnp.concatenate(rows + [jnp.zeros((96, LANES), F32)], axis=0).T
    for k in range(27):
        at = 4 * (16 * (k // 9) + 4 * ((k // 3) % 3) + k % 3)
        gw1_out[k] = rows[at : at + 4, 0:32]
    gb1_out[...] = rows[LANES - 1 : LANES, 0:32]


def solution(mesh):
    n_dp, n_sp = mesh.shape["dp"], mesh.shape["space"]
    per2 = -(-SLOTS // n_dp)
    n_g, n_h = n_dp // 2, 2 * n_sp
    per1 = TILES // n_g
    vm = pl.BlockSpec(memory_space=pltpu.VMEM)
    anywhere = pl.BlockSpec(memory_space=pl.ANY)

    def body(volume, w_first, b_first, w_second, b_second, cotangent):
        parts = pl.pallas_call(
            functools.partial(kernel, n_dp, n_sp),
            out_shape=(
                jax.ShapeDtypeStruct((64, LANES), BF),
                jax.ShapeDtypeStruct((n_g, per1, 8, 128), F32),
                jax.ShapeDtypeStruct((n_dp, per2, 16, 128), BF),
            ),
            in_specs=[anywhere] * 6,
            out_specs=(vm, anywhere, anywhere),
            scratch_shapes=[
                pltpu.VMEM((4, 4, 32, 128), BF),
                pltpu.VMEM((27, 4, 32), BF),
                pltpu.VMEM((1, 32), F32),
                pltpu.VMEM((27, 32, 64), BF),
                pltpu.VMEM((1, 64), F32),
                pltpu.VMEM((64, LANES), BF),
                pltpu.VMEM((128, 6 * LANES), BF),
                pltpu.VMEM((2, 4, 32, 128), BF),
                pltpu.VMEM((2, 6, 6, 16, LANES), BF),
                pltpu.VMEM((256, 128), F32),
                pltpu.VMEM((256, 256), BF),
                pltpu.VMEM((128, 1152), BF),
                pltpu.VMEM((192, 768), BF),
                pltpu.VMEM((8, 8, 32, LANES), F32),
                pltpu.VMEM((2, 4, 32, LANES), BF),
                pltpu.VMEM((2, 4, 32, LANES), BF),
                pltpu.VMEM((4, 4, 128, LANES), BF),
                pltpu.VMEM((2, 4, 64, LANES), BF),
                pltpu.VMEM((2, 2, 64, LANES), BF),
                pltpu.VMEM((2, 2, 64, LANES), BF),
                pltpu.VMEM((2, 4, 256, LANES), BF),
                pltpu.VMEM((4, 128, LANES), F32),
                pltpu.VMEM((256, 8 * LANES), BF),
                pltpu.VMEM((n_dp, per2, 16, 128), F32),
                pltpu.VMEM((n_dp, per2, 16, 128), F32),
                pltpu.VMEM((n_sp, per2, 16, 128), F32),
                pltpu.VMEM((per2, 16, 128), BF),
                pltpu.VMEM((n_g, per1, 8, 128), F32),
                pltpu.VMEM((n_g, per1, 8, 128), F32),
                pltpu.VMEM((n_h, per1, 8, 128), F32),
                pltpu.VMEM((per1, 8, 128), F32),
            ]
            + [pltpu.SemaphoreType.DMA((n,)) for n in (6, 12, 12)],
            compiler_params=pltpu.CompilerParams(collective_id=0, has_side_effects=True),
            name="step",
        )(
            volume.reshape(4, 4, 32, 128),
            w_first.transpose(0, 2, 1),
            b_first.reshape(1, 32),
            w_second.transpose(0, 2, 1),
            b_second.reshape(1, 64),
            cotangent.reshape(64, LANES),
        )
        top, gw1, gb1, gw2, gb2 = pl.pallas_call(
            functools.partial(finish, per2, per1),
            out_shape=(
                jax.ShapeDtypeStruct((64, LANES), BF),
                jax.ShapeDtypeStruct((27, 4, 32), F32),
                jax.ShapeDtypeStruct((1, 32), F32),
                jax.ShapeDtypeStruct((27, 32, 64), F32),
                jax.ShapeDtypeStruct((1, 64), F32),
            ),
            in_specs=[vm] * 3,
            out_specs=(vm,) * 5,
            name="finish",
        )(*parts)
        return (
            top.reshape(1, 64, 1, LANES),
            gw1.transpose(0, 2, 1),
            gb1.reshape(32),
            gw2.transpose(0, 2, 1),
            gb2.reshape(64),
        )

    in_specs = (
        P("dp", None, "space", None, None),
        P(),
        P(),
        P(),
        P(),
        P("dp", None, "space", None),
    )
    out_specs = (P("dp", None, "space", None), P(), P(), P(), P())
    return jax.shard_map(body, mesh=mesh, in_specs=in_specs, out_specs=out_specs, check_vma=False)
```

```python
import functools

import jax
import jax.numpy as jnp
from jax import lax
from jax.experimental import pallas as pl
from jax.experimental.pallas import tpu as pltpu
from jax.sharding import PartitionSpec as P

MESH = pl.DeviceIdType.MESH
BF = jnp.bfloat16
F32 = jnp.float32

LANES = 256
COLS = 32
SLOTS = 28
TILES = 8


def dot(a, b):
    return jnp.dot(a, b, preferred_element_type=F32)


def dot_nt(a, b):
    return lax.dot_general(a, b, (((1,), (1,)), ((), ())), preferred_element_type=F32)


def lane_of(shape):
    return lax.broadcasted_iota(jnp.int32, shape, len(shape) - 1)


def shift_x(v, step):
    lane = lane_of(v.shape)
    moved = pltpu.roll(v, step % LANES, 1)
    edge = 0 if step == 1 else COLS - 1
    return jnp.where(lane % COLS == edge, 0.0, moved)


def shift_y(v, step):
    lane = lane_of(v.shape)
    moved = pltpu.roll(v, (step * COLS) % LANES, 1)
    gone = lane < COLS if step == 1 else lane >= LANES - COLS
    return jnp.where(gone, 0.0, moved)


def leaky(v):
    return jnp.maximum(v, 0.3 * v)


def slope(v):
    return jnp.where(v > 0, 1.0, 0.3)


def column(row):
    n = row.shape[1]
    r = lax.broadcasted_iota(jnp.int32, (n, n), 0)
    c = lax.broadcasted_iota(jnp.int32, (n, n), 1)
    return jnp.sum(jnp.where(r == c, jnp.broadcast_to(row, (n, n)), 0.0), axis=1, keepdims=True)


def window_layer(out, layer, raw, chans, keep):
    wide = []
    for qy in range(2):
        even = raw(2 * qy).astype(F32)
        odd = raw(2 * qy + 1).astype(F32)
        if keep is not None:
            even = jnp.where(keep, even, 0.0)
            odd = jnp.where(keep, odd, 0.0)
        wide.append(jnp.concatenate([shift_x(odd, 1), even, odd, shift_x(even, -1)], axis=0))
    out[layer, 0] = shift_y(wide[1], 1).astype(BF)
    out[layer, 1] = wide[0].astype(BF)
    out[layer, 2] = wide[1].astype(BF)
    out[layer, 3] = shift_y(wide[0], -1).astype(BF)


def kernel(
    n_dp,
    n_sp,
    vol_h,
    w1_h,
    b1_h,
    w2_h,
    b2_h,
    cot_h,
    top_out,
    f1,
    f2,
    vol,
    w1t,
    b1,
    w2t,
    b2,
    cot,
    pick,
    edge_v,
    halo_v,
    ext,
    base_w,
    w1p,
    w2p,
    w2f,
    act1,
    pooled,
    halo_p,
    win2,
    delta2,
    give,
    halo_d,
    win3,
    acc,
    d1,
    g2,
    r2,
    s2,
    t2,
    g1,
    r1,
    s1,
    t1,
    local_sem,
    send_sem,
    recv_sem,
):
    d = lax.axis_index("dp")
    s = lax.axis_index("space")
    left = lax.rem(s + n_sp - 1, n_sp)
    right = lax.rem(s + 1, n_sp)
    has_left = s > 0
    has_right = s < n_sp - 1

    n_g = n_dp // 2
    n_h = 2 * n_sp
    n_z, n_y = n_g // 2, n_sp // 2
    half, g = d // n_g, lax.rem(d, n_g)
    z, core = g // 2, lax.rem(g, 2)
    x_hi, y = s // n_y, lax.rem(s, n_y)
    h = half * n_sp + s

    def ring(step, n):
        return min(step, n - step)

    def peers(x_lo_too, z_too, space_too):
        found = []
        for dx in range(2 if x_lo_too else 1):
            for dz in range(n_z if z_too else 1):
                for dc in range(2 if z_too else 1):
                    for dh in range(2 if space_too else 1):
                        for dy in range(n_y if space_too else 1):
                            if dx + dz + dc + dh + dy == 0:
                                continue
                            hops = ring(dz, n_z) + ring(dy, n_y) + (1 if dx else 2 * dh)
                            found.append((hops, dx, dz, dc, dh, dy))
        found.sort(reverse=True)
        out = []
        for _, dx, dz, dc, dh, dy in found:
            half_to = lax.rem(half + dx, 2)
            g_to = lax.rem(z + dz, n_z) * 2 + lax.rem(core + dc, 2)
            s_to = lax.rem(x_hi + dh, 2) * n_y + lax.rem(y + dy, n_y)
            if space_too:
                at = half_to * n_sp + s_to if x_lo_too else s_to
            else:
                at = half_to * n_g + g_to if x_lo_too else g_to
            device = {}
            if x_lo_too or z_too:
                device["dp"] = half_to * n_g + g_to
            if space_too:
                device["space"] = s_to
            out.append((at, device))
        return out

    dp_peers = peers(True, True, False)
    g_peers = peers(False, True, False)
    h_peers = peers(True, False, True)
    s_peers = peers(False, False, True)

    barrier = pltpu.get_barrier_semaphore()
    for _, device in h_peers + dp_peers:
        pl.semaphore_signal(barrier, inc=1, device_id=device, device_id_type=MESH)
    loads = [
        pltpu.make_async_copy(src, dst, local_sem.at[n])
        for n, (src, dst) in enumerate(
            ((vol_h, vol), (w1_h, w1t), (w2_h, w2t), (b1_h, b1), (b2_h, b2), (cot_h, cot))
        )
    ]
    for copy in loads:
        copy.start()

    for f in range(4):
        r = lax.broadcasted_iota(jnp.int32, (128, LANES), 0)
        c = lane_of((128, LANES)) % COLS
        pick[:, f * LANES : (f + 1) * LANES] = jnp.where(r == 4 * c + f, 1.0, 0.0).astype(BF)
    row = lax.broadcasted_iota(jnp.int32, (64, 512), 0)
    col = lax.broadcasted_iota(jnp.int32, (64, 512), 1)
    gather = jnp.where(
        (row // 16 == col % 4) & ((row % 16) // 4 == col // 128) & (row % 4 == (col % 128) // 32),
        1.0,
        0.0,
    ).astype(BF)
    own_y = (lax.broadcasted_iota(jnp.int32, (256, LANES), 0) % 32) // 4 == lane_of(
        (256, LANES)
    ) // COLS

    def split(planes):
        both = jnp.concatenate(planes, axis=0)
        parts = []
        for f in range(4):
            spread = dot(both, pick[:, f * LANES : (f + 1) * LANES])
            parts.append(jnp.where(own_y, spread, 0.0).astype(BF))
        return [
            dot(gather, jnp.concatenate([part[128 * n : 128 * n + 128] for part in parts], axis=0))
            for n in range(2)
        ]

    def first_layer(layer, cells):
        at = lax.broadcasted_iota(jnp.int32, (64, LANES), 0) % 16
        before = pltpu.roll(shift_x(cells, 1), 64 - 12, 0)
        after = pltpu.roll(shift_x(cells, -1), 12, 0)
        wide = (
            jnp.where(at >= 4, pltpu.roll(cells, 4, 0), before),
            jnp.where(at < 12, pltpu.roll(cells, 64 - 4, 0), after),
        )
        for qx in range(2):
            ext[qx, layer, 0] = shift_y(wide[qx][48:64], 1).astype(BF)
            ext[qx, layer, 1:5] = wide[qx].astype(BF).reshape(4, 16, LANES)
            ext[qx, layer, 5] = shift_y(wide[qx][0:16], -1).astype(BF)

    def halo_copy(src, dst, sem, to):
        return pltpu.make_async_remote_copy(
            src_ref=src,
            dst_ref=dst,
            send_sem=send_sem.at[sem],
            recv_sem=recv_sem.at[sem],
            device_id={"space": to},
            device_id_type=MESH,
        )

    loads[0].wait()
    for pair in ((0, 3), (1, 2)):
        cells = split([vol[:, z].reshape(128, 128) for z in pair])
        for n, z in enumerate(pair):
            if pair == (0, 3):
                edge_v[n] = cells[n].astype(BF)
            first_layer(z + 1, cells[n])

    for copy in loads[1:]:
        copy.wait()
    base_w[...] = jnp.zeros_like(base_w)
    for k in range(27):
        at = 4 * (16 * (k // 9) + 4 * ((k // 3) % 3) + k % 3)
        base_w[at : at + 4, 0:32] = w1t[k].astype(F32)
    base = base_w[...].T[0:32]
    for p in range(8):
        by = 4 * (16 * (p // 4) + 4 * ((p // 2) % 2) + p % 2)
        w1p[32 * p : 32 * p + 32] = (pltpu.roll(base, by, 1) if by else base).astype(BF)
    none = jnp.zeros((32, 64), F32)
    for ac in range(9):
        taps = [w2t[3 * ac + e].astype(F32) for e in range(3)]
        blocks = [
            jnp.concatenate([taps[w] if w < 3 else none, taps[w - 1] if w > 0 else none], axis=1)
            for w in range(4)
        ]
        w2p[:, 128 * ac : 128 * ac + 128] = jnp.concatenate(blocks, axis=0).T.astype(BF)
        down, at = 64 * (2 - ac // 3), 256 * (2 - ac % 3)
        w2f[down : down + 32, at : at + 256] = jnp.concatenate(
            [taps[2], taps[1], taps[0], none], axis=1
        ).astype(BF)
        w2f[down + 32 : down + 64, at : at + 256] = jnp.concatenate(
            [none, taps[2], taps[1], taps[0]], axis=1
        ).astype(BF)
    b1c = column(b1[...])
    b2c = column(b2[...])

    pl.semaphore_wait(barrier, n_h - 1 + n_dp - 1)
    v_left = halo_copy(edge_v.at[0], halo_v.at[1], 0, left)
    v_right = halo_copy(edge_v.at[1], halo_v.at[0], 1, right)
    v_left.start()
    v_right.start()
    v_left.wait_recv()
    v_right.wait_recv()
    for side, keep in ((0, has_left), (1, has_right)):
        first_layer(5 * side, jnp.where(keep, halo_v[side].astype(F32), 0.0))

    def first_window(q):
        qz, qy, qx = q // 4, (q // 2) % 2, q % 2
        return ext[qx, 2 * qz : 2 * qz + 4, 2 * qy : 2 * qy + 4].reshape(256, LANES)

    for qy in range(2):
        for qz in range(2):
            for qx in range(2):
                q = 4 * qz + 2 * qy + qx
                act = dot(w1p[...], first_window(q)).reshape(8, 32, LANES) + b1c[None]
                act1[q] = act
                pooled[qz, 2 * qy + qx] = (jnp.sum(leaky(act), axis=0) * 0.125).astype(BF)
        rows = slice(2 * qy, 2 * qy + 2)
        for qz in range(2):
            halo_copy(
                pooled.at[qz, rows], halo_p.at[1 - qz, rows], 2 + qz, right if qz else left
            ).start()
    p_copies = [halo_copy(pooled.at[qz], halo_p.at[1 - qz], 2 + qz, left) for qz in range(2)]

    for qz in range(2):
        window_layer(win2, 1 + qz, lambda j, qz=qz: pooled[qz, j], 32, None)

    def second_window(pz, py, a0, a1):
        return win2[pz + a0 : pz + a1, py : py + 3].reshape((a1 - a0) * 384, LANES)

    for pz in range(2):
        for py in range(2):
            own = second_window(pz, py, 1 - pz, 3 - pz)
            acc[2 * pz + py] = dot(w2p[:, 384 * (1 - pz) : 384 * (3 - pz)], own)
    grad_top = cot[...].astype(F32) * 0.125
    top = jnp.zeros((64, LANES), F32)
    backs = [[None, None], [None, None]]
    for pz in range(2):
        p_copies[1 - pz].wait_recv()
    for pz in range(2):
        keep = has_right if pz else has_left
        window_layer(win2, 3 * pz, lambda j, pz=pz: halo_p[pz, j], 32, keep)
    for pz in range(2):
        for py in range(2):
            at = 2 * pz
            act = acc[2 * pz + py] + dot(
                w2p[:, 384 * at : 384 * at + 384], second_window(pz, py, at, at + 1)
            )
            for px in range(2):
                one = act[64 * px : 64 * px + 64] + b2c
                top = top + leaky(one)
                delta2[pz, 2 * py + px] = (grad_top * slope(one)).astype(BF)
    for pz in range(2):
        window_layer(win3, pz, lambda j, pz=pz: delta2[pz, j], 64, None)
    for qy in range(2):
        for pz in range(2):
            three = dot(w2f[...], win3[pz, qy : qy + 3].reshape(768, LANES))
            for a in range(3):
                qz, part = 1 + pz - a, three[64 * a : 64 * a + 64]
                if 0 <= qz < 2:
                    there = backs[qz][qy]
                    backs[qz][qy] = part if there is None else there + part
                else:
                    give[pz, qy] = part.astype(BF)
            halo_copy(
                give.at[pz, qy], halo_d.at[1 - pz, qy], 4 + pz, right if pz else left
            ).start()
    d_copies = [halo_copy(give.at[pz], halo_d.at[1 - pz], 4 + pz, left) for pz in range(2)]
    top_out[...] = (top * 0.125).astype(BF)

    both = [(pz, py) for pz in range(2) for py in range(2)]
    there = jnp.concatenate(
        [delta2[pz, 2 * py : 2 * py + 2].reshape(128, LANES) for pz, py in both], axis=1
    )
    sums = dot_nt(jnp.ones((16, 4 * LANES), BF), there)
    low = lane_of((16, 128)) < 64
    per2 = -(-SLOTS // n_dp)
    for a in range(3):
        grad = dot_nt(
            jnp.concatenate([second_window(*b, a, a + 1) for b in both], axis=1), there
        )
        for n in range(9):
            k, at = 9 * a + n, 128 * (n // 3) + 32 * (n % 3)
            here, after = grad[at : at + 32], grad[at + 32 : at + 64]
            first = here[0:16] + pltpu.roll(after[0:16], 64, 1)
            second = pltpu.roll(here[16:32], 64, 1) + after[16:32]
            g2[k // per2, k % per2] = jnp.where(low, first, second)
    g2[27 // per2, 27 % per2] = sums + pltpu.roll(sums, 64, 1)
    for extra in range(SLOTS, per2 * (-(-SLOTS // per2))):
        g2[extra // per2, extra % per2] = jnp.zeros((16, 128), F32)

    def send_all(me, others, src, dst, sem, owners=None):
        for to, device in others:

            def one():
                pltpu.make_async_remote_copy(
                    src_ref=src(to),
                    dst_ref=dst,
                    send_sem=send_sem.at[sem],
                    recv_sem=recv_sem.at[sem],
                    device_id=device,
                    device_id_type=MESH,
                ).start()

            if owners is None:
                one()
            else:
                pl.when(to < owners)(one)

    def all_of(ref, n, sem):
        return pltpu.make_async_remote_copy(
            src_ref=ref.at[0:n],
            dst_ref=ref.at[0:n],
            send_sem=send_sem.at[sem],
            recv_sem=recv_sem.at[sem],
            device_id={"space": right},
            device_id_type=MESH,
        )

    own2 = -(-SLOTS // per2)
    per1 = TILES // n_g

    is_owner = d < own2

    def added(ref, n):
        total = ref[0]
        for j in range(1, n):
            total = total + ref[j]
        return total

    send_all(d, dp_peers, lambda to: g2.at[to], r2.at[d], 6, own2)

    for q in range(8):
        act1[q] = jnp.where(act1[q] > 0, 0.125, 0.3 * 0.125)

    for qz in range(2):
        d_copies[1 - qz].wait_recv()
    grad1 = None
    bias = jnp.zeros((32, LANES), F32)
    for qz in range(2):
        keep = has_right if qz else has_left
        for qy in range(2):
            back = backs[qz][qy] + jnp.where(keep, halo_d[qz, qy].astype(F32), 0.0)
            for qx in range(2):
                q = 4 * qz + 2 * qy + qx
                one = (back[32 * qx : 32 * qx + 32][None] * act1[q]).astype(BF)
                bias = bias + jnp.sum(one.astype(F32), axis=0)
                d1[:, LANES * q : LANES * q + LANES] = one.reshape(256, LANES)
        windows = jnp.concatenate([first_window(4 * qz + j) for j in range(4)], axis=1)
        term = dot_nt(d1[:, 4 * LANES * qz : 4 * LANES * (qz + 1)], windows)
        grad1 = term if grad1 is None else grad1 + term
    fold = grad1[0:32]
    for p in range(1, 8):
        by = 4 * (16 * (p // 4) + 4 * ((p // 2) % 2) + p % 2)
        fold = fold + pltpu.roll(grad1[32 * p : 32 * p + 32], LANES - by, 1)
    bias = jnp.broadcast_to(jnp.sum(bias, axis=1, keepdims=True), (32, LANES))
    fold = jnp.where(lane_of((32, LANES)) == LANES - 1, bias, fold)
    for t in range(8):
        rt, lt = t // 2, t % 2
        g1[t // per1, t % per1] = fold[8 * rt : 8 * rt + 8, 128 * lt : 128 * lt + 128]

    send_all(g, g_peers, lambda to: g1.at[to], r1.at[g], 7)

    @pl.when(is_owner)
    def _():
        r2[d] = g2[d]
        all_of(r2, n_dp - 1, 6).wait_recv()
        s2[s] = added(r2, n_dp)
        send_all(s, s_peers, lambda to: s2.at[s], s2.at[s], 8)

    r1[g] = g1[g]
    all_of(r1, n_g - 1, 7).wait_recv()
    s1[h] = added(r1, n_g)
    send_all(h, h_peers, lambda to: s1.at[h], s1.at[h], 9)

    mine2 = pltpu.make_async_copy(t2, f2.at[d], local_sem.at[0])
    mine1 = pltpu.make_async_copy(t1, f1.at[g], local_sem.at[1])

    @pl.when(is_owner)
    def _():
        all_of(s2, n_sp - 1, 8).wait_recv()
        t2[...] = added(s2, n_sp).astype(BF)
        send_all(d, dp_peers, lambda to: t2, f2.at[d], 10)
        mine2.start()

    all_of(s1, n_h - 1, 9).wait_recv()
    t1[...] = added(s1, n_h)
    send_all(g, g_peers, lambda to: t1, f1.at[g], 11)
    mine1.start()

    for copy in [v_left, v_right] + p_copies + d_copies:
        copy.wait_send()
    all_of(g1, n_g - 1, 7).wait_send()
    all_of(s1, n_h - 1, 9).wait_send()

    @pl.when(is_owner)
    def _():
        all_of(g2, own2 - 1, 6).wait_send()
        all_of(s2, n_sp - 1, 8).wait_send()
        mine2.wait()
        all_of(f2, n_dp - 1, 10).wait_send()
        all_of(f2, own2 - 1, 10).wait_recv()

    @pl.when(jnp.logical_not(is_owner))
    def _():
        all_of(g2, own2, 6).wait_send()
        all_of(f2, own2, 10).wait_recv()

    mine1.wait()
    all_of(f1, n_g - 1, 11).wait_send()
    all_of(f1, n_g - 1, 11).wait_recv()


def finish(per2, per1, top, f1, f2, top_out, gw1_out, gb1_out, gw2_out, gb2_out):
    top_out[...] = top[...]
    for k in range(27):
        both = f2[k // per2, k % per2].astype(F32)
        gw2_out[k, 0:16] = both[:, 0:64]
        gw2_out[k, 16:32] = pltpu.roll(both, 64, 1)[:, 0:64]
    gb2_out[...] = f2[27 // per2, 27 % per2].astype(F32)[0:1, 0:64]
    rows = []
    for rt in range(4):
        tiles = [f1[(2 * rt + lt) // per1, (2 * rt + lt) % per1] for lt in range(2)]
        rows.append(jnp.concatenate(tiles, axis=1))
    rows = jnp.concatenate(rows + [jnp.zeros((96, LANES), F32)], axis=0).T
    for k in range(27):
        at = 4 * (16 * (k // 9) + 4 * ((k // 3) % 3) + k % 3)
        gw1_out[k] = rows[at : at + 4, 0:32]
    gb1_out[...] = rows[LANES - 1 : LANES, 0:32]


def solution(mesh):
    n_dp, n_sp = mesh.shape["dp"], mesh.shape["space"]
    per2 = -(-SLOTS // n_dp)
    n_g, n_h = n_dp // 2, 2 * n_sp
    per1 = TILES // n_g
    vm = pl.BlockSpec(memory_space=pltpu.VMEM)
    anywhere = pl.BlockSpec(memory_space=pl.ANY)

    def body(volume, w_first, b_first, w_second, b_second, cotangent):
        parts = pl.pallas_call(
            functools.partial(kernel, n_dp, n_sp),
            out_shape=(
                jax.ShapeDtypeStruct((64, LANES), BF),
                jax.ShapeDtypeStruct((n_g, per1, 8, 128), F32),
                jax.ShapeDtypeStruct((n_dp, per2, 16, 128), BF),
            ),
            in_specs=[anywhere] * 6,
            out_specs=(vm, anywhere, anywhere),
            scratch_shapes=[
                pltpu.VMEM((4, 4, 32, 128), BF),
                pltpu.VMEM((27, 4, 32), BF),
                pltpu.VMEM((1, 32), F32),
                pltpu.VMEM((27, 32, 64), BF),
                pltpu.VMEM((1, 64), F32),
                pltpu.VMEM((64, LANES), BF),
                pltpu.VMEM((128, 4 * LANES), BF),
                pltpu.VMEM((2, 64, LANES), BF),
                pltpu.VMEM((2, 64, LANES), BF),
                pltpu.VMEM((2, 6, 6, 16, LANES), BF),
                pltpu.VMEM((256, 128), F32),
                pltpu.VMEM((256, 256), BF),
                pltpu.VMEM((128, 1152), BF),
                pltpu.VMEM((192, 768), BF),
                pltpu.VMEM((8, 8, 32, LANES), F32),
                pltpu.VMEM((2, 4, 32, LANES), BF),
                pltpu.VMEM((2, 4, 32, LANES), BF),
                pltpu.VMEM((4, 4, 128, LANES), BF),
                pltpu.VMEM((2, 4, 64, LANES), BF),
                pltpu.VMEM((2, 2, 64, LANES), BF),
                pltpu.VMEM((2, 2, 64, LANES), BF),
                pltpu.VMEM((2, 4, 256, LANES), BF),
                pltpu.VMEM((4, 128, LANES), F32),
                pltpu.VMEM((256, 8 * LANES), BF),
                pltpu.VMEM((n_dp, per2, 16, 128), F32),
                pltpu.VMEM((n_dp, per2, 16, 128), F32),
                pltpu.VMEM((n_sp, per2, 16, 128), F32),
                pltpu.VMEM((per2, 16, 128), BF),
                pltpu.VMEM((n_g, per1, 8, 128), F32),
                pltpu.VMEM((n_g, per1, 8, 128), F32),
                pltpu.VMEM((n_h, per1, 8, 128), F32),
                pltpu.VMEM((per1, 8, 128), F32),
            ]
            + [pltpu.SemaphoreType.DMA((n,)) for n in (6, 12, 12)],
            compiler_params=pltpu.CompilerParams(collective_id=0, has_side_effects=True),
            name="step",
        )(
            volume.reshape(4, 4, 32, 128),
            w_first.transpose(0, 2, 1),
            b_first.reshape(1, 32),
            w_second.transpose(0, 2, 1),
            b_second.reshape(1, 64),
            cotangent.reshape(64, LANES),
        )
        top, gw1, gb1, gw2, gb2 = pl.pallas_call(
            functools.partial(finish, per2, per1),
            out_shape=(
                jax.ShapeDtypeStruct((64, LANES), BF),
                jax.ShapeDtypeStruct((27, 4, 32), F32),
                jax.ShapeDtypeStruct((1, 32), F32),
                jax.ShapeDtypeStruct((27, 32, 64), F32),
                jax.ShapeDtypeStruct((1, 64), F32),
            ),
            in_specs=[vm] * 3,
            out_specs=(vm,) * 5,
            name="finish",
        )(*parts)
        return (
            top.reshape(1, 64, 1, LANES),
            gw1.transpose(0, 2, 1),
            gb1.reshape(32),
            gw2.transpose(0, 2, 1),
            gb2.reshape(64),
        )

    in_specs = (
        P("dp", None, "space", None, None),
        P(),
        P(),
        P(),
        P(),
        P("dp", None, "space", None),
    )
    out_specs = (P("dp", None, "space", None), P(), P(), P(), P())
    return jax.shard_map(body, mesh=mesh, in_specs=in_specs, out_specs=out_specs, check_vma=False)
```
